32 devices in a mesh: seq: 16 (over z, x, core), exp: 2 (over y).
Axes of the slice: x: 2, y: 2, z: 4, core: 2. Of those that a mesh axis runs over, the one named last changes fastest.
Arguments:
- tokens: bfloat16 [30720, 1024], P('seq'), may hold values from -24 to 24
- slot_embed: bfloat16 [1024, 512], P(None, 'exp'), may hold values from -3 to 3
- w_in: bfloat16 [32, 1024, 4096], P('exp', None, 'seq'), may hold values from -0.375 to 0.375
- w_out: bfloat16 [32, 4096, 1024], P('exp', 'seq'), may hold values from -0.125 to 0.125
Outputs:
- mixed_out: bfloat16 [30720, 1024], P('seq', 'exp')
The draws below stay inside these ranges and needn't reach their ends.
All inputs are finite; a program needn't handle non-finite values.
Results may differ from the reference program's by a relative error of at most 0.012.
Values may be sent and summed in bfloat16 or wider, within the bound.
A program may use at most 64 MiB of HBM per device.

```python
import math
import jax
import jax.numpy as jnp
from jax import lax

D = 1024
HID = 4096
SLOT_EXP = 16
TOK_DEV = 1920
TOKENS = 30720
EXPERTS = 32
SLOTS = 512
N_SEQ = 16
N_EXP = 2


def embed_table(key):
    fraction = jnp.arange(SLOTS, dtype=jnp.float32) / max(SLOTS - 1, 1)
    base_scale = 3.0 / math.sqrt(D) * (0.9 + 0.25 * fraction)
    normals = jnp.clip(jax.random.normal(jax.random.fold_in(key, 11), (D, SLOTS), jnp.float32), -6.0, 6.0)
    table = normals * base_scale[None, :]
    return table


def draw_slot_embed(key, part):
    table = embed_table(key)
    return table.astype(jnp.bfloat16)


def draw_tokens(key, part):
    position = jnp.arange(TOKENS, dtype=jnp.float32) / max(TOKENS - 1, 1)
    row_scale = 0.9 + 0.2 * position
    entries = jnp.clip(jax.random.normal(jax.random.fold_in(key, 21), (TOKENS, D), jnp.float32), -6.0, 6.0)
    values = entries * row_scale[:, None]
    return values.astype(jnp.bfloat16)


def steps_of(key, extent, pieces, low, top_value):
    level = 1.0
    for axis_at, shards_of in pieces:
        draws = jax.random.uniform(jax.random.fold_in(jax.random.fold_in(key, 6), axis_at), (shards_of,), jnp.float32, low / len(pieces), top_value / len(pieces))
        level = level * jnp.repeat(jnp.exp(draws), extent[axis_at] // shards_of).reshape((-1,) + (1,) * (len(extent) - 1 - axis_at))
    return level


def scatter_about(own_key, shape, width, reach, pieces=(), kind=jnp.bfloat16):
    factor_of = steps_of(own_key, shape, pieces, -0.22, 0.18) if pieces else 1.0
    values = jax.random.normal(own_key, shape, jnp.float32) * width * factor_of
    return jnp.minimum(jnp.maximum(values, -reach), reach).astype(kind)


def setup_inputs(seed: int = 0) -> dict:
    keys = jax.random.split(jax.random.key(seed), 5)
    return {
        "tokens": draw_tokens(jax.random.fold_in(keys[4], 71), 0),
        "slot_embed": draw_slot_embed(jax.random.fold_in(keys[4], 71), 0),
        "w_in": scatter_about(keys[2], (EXPERTS, D, HID), (D // 4) ** -0.5, 0.375, ((0, 2), (2, 16))),
        "w_out": scatter_about(keys[3], (EXPERTS, HID, D), (HID // 2) ** -0.5, 0.125, ((0, 2), (1, 16))),
    }


def gelu_tanh(values):
    return 0.5 * values * (1.0 + jnp.tanh(0.7978845608028654 * (values + 0.044715 * values * values * values)))


def reference(tokens, slot_embed, w_in, w_out):
    group_size = SLOTS // N_EXP
    blocks = slot_embed.reshape(D, N_EXP, group_size).transpose(1, 0, 2)

    def dispatch_block(embed_block):
        logits = jnp.dot(tokens, embed_block, preferred_element_type=jnp.float32)
        col_peak = jnp.max(logits, axis=0)
        weights = jnp.exp(logits - col_peak[None, :])
        col_total = jnp.sum(weights, axis=0)
        dispatch = (weights / col_total[None, :]).astype(jnp.bfloat16)
        summed = lax.dot_general(dispatch, tokens, (((0,), (0,)), ((), ())), preferred_element_type=jnp.float32)
        return summed.astype(jnp.bfloat16)

    slot_in = lax.map(dispatch_block, blocks).reshape(EXPERTS, SLOT_EXP, D)

    def expert_apply(operands):
        inputs, first, second = operands
        hidden = gelu_tanh(jnp.dot(inputs, first, preferred_element_type=jnp.float32)).astype(jnp.bfloat16)
        return jnp.dot(hidden, second, preferred_element_type=jnp.float32).astype(jnp.bfloat16)

    slot_out = lax.map(expert_apply, (slot_in, w_in, w_out)).reshape(N_EXP, group_size, D)
    row_blocks = tokens.reshape(N_SEQ, TOK_DEV, D)

    def combine_block(row_block):
        logits = jnp.dot(row_block, slot_embed, preferred_element_type=jnp.float32)
        row_peak = jnp.max(logits, axis=1)
        weights = jnp.exp(logits - row_peak[:, None])
        row_total = jnp.sum(weights, axis=1)
        combine = (weights / row_total[:, None]).astype(jnp.bfloat16)
        part_blocks = combine.reshape(TOK_DEV, N_EXP, group_size).astype(jnp.float32)
        group_mix = jnp.einsum("bgs,gsd->bgd", part_blocks, slot_out.astype(jnp.float32)).astype(jnp.bfloat16)
        group_mix = lax.optimization_barrier(group_mix)
        return jnp.sum(group_mix.astype(jnp.float32), axis=1).astype(jnp.bfloat16)

    return lax.map(combine_block, row_blocks).reshape(TOKENS, D)
```

```python
import functools

import jax
import jax.numpy as jnp
from jax import lax
from jax.experimental import pallas as pl
from jax.experimental.pallas import tpu as pltpu
from jax.sharding import PartitionSpec as P

MESH = pl.DeviceIdType.MESH
F32 = jnp.float32
BF16 = jnp.bfloat16


def gelu_tanh(v):
    return 0.5 * v * (1.0 + jnp.tanh(0.7978845608028654 * (v + 0.044715 * v * v * v)))


def rcopy(src, dst, send, recv, dev):
    return pltpu.make_async_remote_copy(
        src_ref=src, dst_ref=dst, send_sem=send, recv_sem=recv, device_id=dev, device_id_type=MESH
    )


def column(row, slots):
    return jnp.transpose(jnp.broadcast_to(row, (128, slots)))


def kernel(
    n_seq, n_exp, slot_exp, tok_hbm, emb_hbm, win_hbm, wout_hbm, out,
    tok, emb, embt, win, wout, logt, pt, acc, comb, m1, l1, s2, fac, wide, tot,
    snd1, rcv1, snd2, rcv2, ag, keep, snd3, rcv3, snd4, rcv4, so,
    sem_tok, sem_in, sem_w, sem_emb, sem_er, sem_m, sem_snd,
    sem_s, sem_1, sem_2, sem_ag, sem_fw, sem_3, sem_4, sem_a, sem_af,
):
    n_chip = n_seq // 2
    count, features = tok.shape
    slots = embt.shape[0]
    rows = slots // n_seq
    half = slots // 2
    cols = features // n_exp
    tile = 256
    n_tile = features // tile
    n_cut = so.shape[0]
    wide_cut = cols // n_cut
    mirror = n_chip // 2
    me = lax.axis_index("seq")
    mine = lax.axis_index("exp")
    chip = me // 2
    core = lax.rem(me, 2)
    other = 1 - core
    partner = {"seq": chip * 2 + other}
    pending = []

    def near(r):
        return chip_ids[r]

    chip_ids = [chip]
    for r in range(1, n_chip):
        mate, bit = chip, 1
        while bit < n_chip:
            if r & bit:
                mate = mate + bit * (1 - 2 * lax.rem(chip // bit, 2))
            bit *= 2
        chip_ids.append(mate)
    far_first = list(range(n_chip - 1, 0, -1))

    def peer(r):
        return {"seq": near(r) * 2 + core}

    def group_at(s):
        return lax.rem(mine + s, n_exp)

    def across(r, s):
        return {"seq": near(r) * 2 + core, "exp": group_at(s)}

    def go(cp):
        cp.start()
        pending.append(cp)

    def landed(view, sem):
        rcopy(view, view, sem, sem, partner).wait_recv()

    def drained(view, sem):
        rcopy(view, view, sem, sem, partner).wait_send()

    barrier = pltpu.get_barrier_semaphore()
    for s in range(n_exp):
        for r in range(n_chip):
            if r or s:
                pl.semaphore_signal(barrier, inc=1, device_id=across(r, s), device_id_type=MESH)
    pl.semaphore_signal(barrier, inc=1, device_id=partner, device_id_type=MESH)

    emb_in = pltpu.make_async_copy(emb_hbm, emb.at[0], sem_in)
    emb_in.start()
    chunks = []
    at = 0
    while at < count:
        size = min(512, count - at)
        cp = pltpu.make_async_copy(tok_hbm.at[pl.ds(at, size)], tok.at[pl.ds(at, size)], sem_tok.at[len(chunks)])
        cp.start()
        chunks.append((at, size, cp))
        at += size

    emb_in.wait()
    for q in range(n_tile):
        embt[:, q * tile:(q + 1) * tile] = jnp.transpose(emb[0, q * tile:(q + 1) * tile, :])
    peak = None
    deep = features // 2

    def part_of(which):
        return pl.ds(pl.multiple_of(which * deep, deep), deep)

    def emb_copy(r):
        there = emb.at[r, part_of(core)]
        return rcopy(emb.at[0, part_of(core)], there, sem_emb.at[0, r], sem_emb.at[1, r], {"exp": group_at(r)})

    def emb_relay(r, which):
        there = emb.at[r, part_of(which)]
        return rcopy(there, there, sem_er.at[0, r], sem_er.at[1, r], partner)

    for at, size, cp in chunks:
        cp.wait()
        lt = lax.dot_general(
            embt[...], tok[at:at + size, :], (((1,), (1,)), ((), ())), preferred_element_type=F32
        )
        logt[:, at:at + size] = lt
        top = jnp.max(lt, axis=1, keepdims=True)
        peak = top if peak is None else jnp.maximum(peak, top)
        if at == 0:
            pl.semaphore_wait(barrier, n_chip * n_exp)
            for r in range(1, n_exp):
                go(emb_copy(r))
    win_in = pltpu.make_async_copy(win_hbm, win, sem_w.at[0])
    wout_in = pltpu.make_async_copy(wout_hbm, wout, sem_w.at[1])
    win_in.start()
    wout_in.start()
    m1[0] = jnp.transpose(jnp.broadcast_to(peak, (slots, 128)))[0:1, :]
    m_copy = rcopy(m1.at[0], m1.at[1], sem_m.at[0, 0], sem_m.at[1, 0], partner)
    go(m_copy)

    total = None
    for at, size, _ in chunks:
        w = jnp.exp(logt[:, at:at + size] - peak)
        pt[:, at:at + size] = w.astype(BF16)
        part = jnp.sum(w, axis=1, keepdims=True)
        total = part if total is None else total + part
    l1[0] = jnp.transpose(jnp.broadcast_to(total, (slots, 128)))[0:1, :]
    l_copy = rcopy(l1.at[0], l1.at[1], sem_m.at[0, 1], sem_m.at[1, 1], partner)
    go(l_copy)

    def half_rows(which):
        return pl.ds(pl.multiple_of(which * half, half), half)

    def cut(q):
        return pl.ds(q * tile, tile)

    for q in range(n_tile):
        acc[:, q * tile:(q + 1) * tile] = jnp.dot(
            pt[...], tok[:, q * tile:(q + 1) * tile], preferred_element_type=F32
        )
        snd1[q] = acc[half_rows(other), q * tile:(q + 1) * tile].astype(BF16)
        rcopy(snd1.at[q], rcv1.at[q], sem_snd.at[1], sem_1.at[q], partner).start()
    m_copy.wait_recv()
    top_pair = jnp.maximum(m1[0], m1[1])
    shrink = [jnp.exp(m1[i] - top_pair) for i in range(2)]
    for i in range(2):
        fac[i] = column(shrink[i], slots)
    l_copy.wait_recv()
    s2[0, 0] = top_pair
    s2[0, 1] = l1[0] * shrink[0] + l1[1] * shrink[1]
    for r in far_first:
        rcopy(s2.at[0], s2.at[r], sem_snd.at[0], sem_s, peer(r)).start()
    own_fac = fac[0, half_rows(core), :][:, 0:1]
    got_fac = fac[1, half_rows(core), :][:, 0:1]
    for q in range(n_tile):
        landed(rcv1.at[q], sem_1.at[q])
        both = acc[half_rows(core), q * tile:(q + 1) * tile] * own_fac + rcv1[q].astype(F32) * got_fac
        snd2[:, :, q * tile:(q + 1) * tile] = both.reshape(n_chip, rows, tile).astype(BF16)
        for r in far_first:
            rcopy(
                snd2.at[near(r), :, cut(q)], rcv2.at[r, :, cut(q)], sem_snd.at[2], sem_2.at[q], peer(r)
            ).start()

    landed(s2.at[pl.ds(1, n_chip - 1)], sem_s)
    top_all = functools.reduce(jnp.maximum, [s2[r, 0] for r in range(n_chip)])
    factors = [jnp.exp(s2[r, 0] - top_all) for r in range(n_chip)]
    grand = functools.reduce(jnp.add, [s2[r, 1] * factors[r] for r in range(n_chip)])
    wide[...] = jnp.zeros_like(wide)
    for r in range(n_chip):
        wide[r:r + 1, :] = factors[r] / grand
    tot[...] = jnp.transpose(wide[...])
    piece = core * n_chip + chip
    weight = tot[pl.ds(pl.multiple_of(piece * rows, rows), rows), :]
    for q in range(n_tile):
        landed(rcv2.at[pl.ds(1, n_chip - 1), :, cut(q)], sem_2.at[q])
        mine_sum = snd2[chip, :, q * tile:(q + 1) * tile].astype(F32) * weight[:, 0:1]
        for r in range(1, n_chip):
            mine_sum = mine_sum + rcv2[r, :, q * tile:(q + 1) * tile].astype(F32) * weight[:, r:r + 1]
        ag[piece, :, q * tile:(q + 1) * tile] = mine_sum.astype(BF16)
        span = ag.at[piece, :, cut(q)]
        rcopy(span, span, sem_snd.at[4], sem_fw.at[0], partner).start()
        for r in range(mirror - 1, 0, -1):
            rcopy(span, span, sem_snd.at[3], sem_ag.at[r], peer(r)).start()
    for r in range(mirror, n_chip):
        rcopy(ag.at[piece], ag.at[piece], sem_snd.at[3], sem_ag.at[r], peer(r)).start()

    for r in range(1, n_exp):
        emb_copy(r).wait_recv()
        go(emb_relay(r, core))
    win_in.wait()
    wout_in.wait()

    def expert(p):
        e = (p * rows) // slot_exp
        h = gelu_tanh(jnp.dot(ag[p], win[e], preferred_element_type=F32)).astype(BF16)
        return jnp.dot(h, wout[e], preferred_element_type=F32)

    for rs in (range(mirror), range(mirror, n_chip)):
        for r in rs:
            p = core * n_chip + near(r)
            if r:
                landed(ag.at[p], sem_ag.at[r])
                rcopy(ag.at[p], ag.at[p], sem_snd.at[4], sem_fw.at[r], partner).start()
        for r in rs:
            keep[r] = expert(core * n_chip + near(r))
        for r in rs:
            p = other * n_chip + near(r)
            landed(ag.at[p], sem_fw.at[r])
            snd3[r] = expert(p).astype(BF16)
            rcopy(snd3.at[r], rcv3.at[r], sem_snd.at[5], sem_3.at[r], partner).start()
        for r in rs:
            landed(rcv3.at[r], sem_3.at[r])
            y = (keep[r] + rcv3[r].astype(F32)).astype(BF16)
            for q in range(n_exp):
                for h in range(n_cut):
                    low = q * cols + h * wide_cut
                    snd4[h, q * n_chip + (r ^ mirror)] = y[:, low:low + wide_cut]
        for h in range(n_cut):
            for r in rs:
                d = r ^ mirror
                for s in range(n_exp):
                    if d or s:
                        rcopy(
                            snd4.at[h, group_at(s) * n_chip + d], rcv4.at[h, s * n_chip + d],
                            sem_snd.at[6 + h], sem_4.at[h], across(d, s),
                        ).start()

    step = next(s for s in (384, 256, 128, 64, 32, 16) if count % s == 0)

    def combine(i, carry):
        here = pl.ds(pl.multiple_of(i * step, step), step)
        rows_in = tok[here, :]
        parts = [jnp.dot(rows_in, emb[r], preferred_element_type=F32) for r in range(n_exp)]
        top = jnp.max(functools.reduce(jnp.maximum, parts), axis=1, keepdims=True)
        parts = [jnp.exp(v - top) for v in parts]
        full = jnp.sum(functools.reduce(jnp.add, parts), axis=1, keepdims=True)
        inv = 1.0 / full
        for r in range(n_exp):
            comb[here, r * slots:(r + 1) * slots] = (parts[r] * inv).astype(BF16)
        return carry

    for r in range(1, n_exp):
        emb_relay(r, other).wait_recv()
    n_step = count // step
    early = n_step * 3 // 5
    lax.fori_loop(0, early, combine, 0)

    every = pl.ds(0, n_exp)
    cuts = pl.ds(0, n_cut)
    homed = core * n_chip + near(mirror)
    for h in range(n_cut):
        landed(rcv4.at[h, pl.ds(1, n_chip * n_exp - 1)], sem_4.at[h])
        for s in range(n_exp):
            sums = snd4[h, mine * n_chip].astype(F32) if s == 0 else None
            for d in range(n_chip):
                if d or s:
                    got = rcv4[h, s * n_chip + d].astype(F32)
                    sums = got if sums is None else sums + got
            so[h, s, homed] = sums.astype(BF16)
        span = so.at[h, every, homed]
        for r in far_first:
            rcopy(span, span, sem_snd.at[6 + n_cut], sem_a.at[h, r], peer(r)).start()
        rcopy(span, span, sem_snd.at[7 + n_cut], sem_af.at[h], partner).start()
    lax.fori_loop(early, n_step, combine, 0)
    for h in range(n_cut):
        for r in range(1, n_chip):
            span = so.at[h, every, core * n_chip + near(r ^ mirror)]
            landed(span, sem_a.at[h, r])
            rcopy(span, span, sem_snd.at[7 + n_cut], sem_af.at[h], partner).start()
    flat = (n_exp * slots, wide_cut)
    for h in range(n_cut):
        landed(so.at[h, every, pl.ds(other * n_chip, n_chip)], sem_af.at[h])
        for i in range(count // step):
            here = pl.ds(i * step, step)
            table = so[h].reshape(flat) if rows % 16 == 0 else so[h].astype(F32).reshape(flat).astype(BF16)
            mixed = jnp.dot(comb[here, :], table, preferred_element_type=F32).astype(BF16)
            out[here, h * wide_cut:(h + 1) * wide_cut] = mixed
    for cp in pending:
        cp.wait_send()
    drained(s2.at[pl.ds(1, n_chip - 1)], sem_snd.at[0])
    drained(snd1, sem_snd.at[1])
    drained(snd2.at[pl.ds(0, n_chip - 1)], sem_snd.at[2])
    drained(ag.at[pl.ds(0, n_chip - 1)], sem_snd.at[3])
    drained(ag.at[pl.ds(0, n_chip)], sem_snd.at[4])
    drained(snd3, sem_snd.at[5])
    for h in range(n_cut):
        drained(snd4.at[h, pl.ds(0, n_chip * n_exp - 1)], sem_snd.at[6 + h])
    drained(so.at[cuts, every, pl.ds(0, n_chip - 1)], sem_snd.at[6 + n_cut])
    drained(so.at[cuts, every, pl.ds(0, n_chip)], sem_snd.at[7 + n_cut])


def solution(mesh):
    n_seq, n_exp = mesh.shape["seq"], mesh.shape["exp"]
    n_chip = n_seq // 2

    def on_device(tokens, slot_embed, w_in, w_out):
        count, features = tokens.shape
        slots = slot_embed.shape[1]
        experts, _, hid = w_in.shape
        slot_exp = slots // experts
        rows = slots // n_seq
        half = slots // 2
        cols = features // n_exp
        n_tile = features // 256
        n_cut = 2 if cols % 256 == 0 else 1
        room = 49 * 1024 * 1024
        dma = pltpu.SemaphoreType.DMA
        vmem = pltpu.VMEM
        anywhere = pl.BlockSpec(memory_space=pltpu.HBM)
        return pl.pallas_call(
            functools.partial(kernel, n_seq, n_exp, slot_exp),
            out_shape=jax.ShapeDtypeStruct((count, cols), BF16),
            in_specs=[anywhere] * 4,
            out_specs=pl.BlockSpec(memory_space=pltpu.VMEM),
            scratch_shapes=[
                vmem((count, features), BF16),
                vmem((n_exp, features, slots), BF16),
                vmem((slots, features), BF16),
                vmem(w_in.shape, BF16),
                vmem(w_out.shape, BF16),
                vmem((slots, count), F32),
                vmem((slots, count), BF16),
                vmem((slots, features), F32),
                vmem((count, n_exp * slots), BF16),
                vmem((2, 1, slots), F32),
                vmem((2, 1, slots), F32),
                vmem((n_chip, 2, 1, slots), F32),
                vmem((2, slots, 128), F32),
                vmem((128, slots), F32),
                vmem((slots, 128), F32),
                vmem((n_tile, half, 256), BF16),
                vmem((n_tile, half, 256), BF16),
                vmem((n_chip, rows, features), BF16),
                vmem((n_chip, rows, features), BF16),
                vmem((n_seq, rows, features), BF16),
                vmem((n_chip, rows, features), F32),
                vmem((n_chip, rows, features), BF16),
                vmem((n_chip, rows, features), BF16),
                vmem((n_cut, n_exp * n_chip, rows, cols // n_cut), BF16),
                vmem((n_cut, n_exp * n_chip, rows, cols // n_cut), BF16),
                vmem((n_cut, n_exp, n_seq, rows, cols // n_cut), BF16),
                dma((-(-count // 512),)),
                dma,
                dma((2,)),
                dma((2, n_exp)),
                dma((2, n_exp)),
                dma((2, 2)),
                dma((8 + n_cut,)),
                dma,
                dma((n_tile,)),
                dma((n_tile,)),
                dma((n_chip,)),
                dma((n_chip,)),
                dma((n_chip,)),
                dma((n_cut,)),
                dma((n_cut, n_chip)),
                dma((n_cut,)),
            ],
            compiler_params=pltpu.CompilerParams(
                collective_id=0, has_side_effects=True, vmem_limit_bytes=room
            ),
        )(tokens, slot_embed, w_in, w_out)

    placed = (P("seq", None), P(None, "exp"), P("exp", None, "seq"), P("exp", "seq", None))
    return jax.shard_map(
        on_device, mesh=mesh, in_specs=placed, out_specs=P("seq", "exp"), check_vma=False
    )
```

```python
import functools

import jax
import jax.numpy as jnp
from jax import lax
from jax.experimental import pallas as pl
from jax.experimental.pallas import tpu as pltpu
from jax.sharding import PartitionSpec as P

MESH = pl.DeviceIdType.MESH
F32 = jnp.float32
BF16 = jnp.bfloat16


def gelu_tanh(v):
    return 0.5 * v * (1.0 + jnp.tanh(0.7978845608028654 * (v + 0.044715 * v * v * v)))


def rcopy(src, dst, send, recv, dev):
    return pltpu.make_async_remote_copy(
        src_ref=src, dst_ref=dst, send_sem=send, recv_sem=recv, device_id=dev, device_id_type=MESH
    )


def column(row, slots):
    return jnp.transpose(jnp.broadcast_to(row, (128, slots)))


def kernel(
    n_seq, n_exp, slot_exp, tok_hbm, emb_hbm, win_hbm, wout_hbm, out,
    tok, emb, embt, win, wout, logt, pt, acc, comb, m1, l1, s2, fac, wide, tot,
    snd1, rcv1, snd2, rcv2, ag, keep, snd3, rcv3, snd4, rcv4, xs, xr, so,
    sem_tok, sem_in, sem_w, sem_emb, sem_er, sem_m, sem_snd,
    sem_s, sem_1, sem_2, sem_ag, sem_fw, sem_3, sem_4, sem_x, sem_a, sem_af,
):
    n_chip = n_seq // 2
    count, features = tok.shape
    slots = embt.shape[0]
    rows = slots // n_seq
    half = slots // 2
    cols = features // n_exp
    tile = 256
    n_tile = features // tile
    n_cut = so.shape[0]
    wide_cut = cols // n_cut
    mirror = n_chip // 2
    me = lax.axis_index("seq")
    mine = lax.axis_index("exp")
    chip = me // 2
    core = lax.rem(me, 2)
    other = 1 - core
    partner = {"seq": chip * 2 + other}
    pending = []

    def near(r):
        return chip_ids[r]

    chip_ids = [chip]
    for r in range(1, n_chip):
        mate, bit = chip, 1
        while bit < n_chip:
            if r & bit:
                mate = mate + bit * (1 - 2 * lax.rem(chip // bit, 2))
            bit *= 2
        chip_ids.append(mate)
    far_first = list(range(n_chip - 1, 0, -1))

    def peer(r):
        return {"seq": near(r) * 2 + core}

    def group_at(s):
        return lax.rem(mine + s, n_exp)

    def across(r, s):
        return {"seq": near(r) * 2 + core, "exp": group_at(s)}

    def go(cp):
        cp.start()
        pending.append(cp)

    def landed(view, sem):
        rcopy(view, view, sem, sem, partner).wait_recv()

    def drained(view, sem):
        rcopy(view, view, sem, sem, partner).wait_send()

    emb_in = pltpu.make_async_copy(emb_hbm, emb.at[0], sem_in)
    emb_in.start()
    chunks = []
    at = 0
    while at < count:
        size = min(512, count - at)
        cp = pltpu.make_async_copy(tok_hbm.at[pl.ds(at, size)], tok.at[pl.ds(at, size)], sem_tok.at[len(chunks)])
        cp.start()
        chunks.append((at, size, cp))
        at += size

    barrier = pltpu.get_barrier_semaphore()
    for s in range(n_exp):
        for r in range(n_chip):
            if r or s:
                pl.semaphore_signal(barrier, inc=1, device_id=across(r, s), device_id_type=MESH)
    pl.semaphore_signal(barrier, inc=1, device_id=partner, device_id_type=MESH)

    emb_in.wait()
    for q in range(n_tile):
        embt[:, q * tile:(q + 1) * tile] = jnp.transpose(emb[0, q * tile:(q + 1) * tile, :])
    peak = None
    deep = features // 2

    def part_of(which):
        return pl.ds(pl.multiple_of(which * deep, deep), deep)

    def emb_copy(r):
        there = emb.at[r, part_of(core)]
        return rcopy(emb.at[0, part_of(core)], there, sem_emb.at[0, r], sem_emb.at[1, r], {"exp": group_at(r)})

    def emb_relay(r, which):
        there = emb.at[r, part_of(which)]
        return rcopy(there, there, sem_er.at[0, r], sem_er.at[1, r], partner)

    for at, size, cp in chunks:
        cp.wait()
        lt = lax.dot_general(
            embt[...], tok[at:at + size, :], (((1,), (1,)), ((), ())), preferred_element_type=F32
        )
        logt[:, at:at + size] = lt
        top = jnp.max(lt, axis=1, keepdims=True)
        peak = top if peak is None else jnp.maximum(peak, top)
        if at == 0:
            pl.semaphore_wait(barrier, n_chip * n_exp)
            for r in range(1, n_exp):
                go(emb_copy(r))
    win_in = pltpu.make_async_copy(win_hbm, win, sem_w.at[0])
    wout_in = pltpu.make_async_copy(wout_hbm, wout, sem_w.at[1])
    win_in.start()
    wout_in.start()
    m1[0] = jnp.transpose(jnp.broadcast_to(peak, (slots, 128)))[0:1, :]
    m_copy = rcopy(m1.at[0], m1.at[1], sem_m.at[0, 0], sem_m.at[1, 0], partner)
    go(m_copy)

    total = None
    for at, size, _ in chunks:
        w = jnp.exp(logt[:, at:at + size] - peak)
        pt[:, at:at + size] = w.astype(BF16)
        part = jnp.sum(w, axis=1, keepdims=True)
        total = part if total is None else total + part
    l1[0] = jnp.transpose(jnp.broadcast_to(total, (slots, 128)))[0:1, :]
    l_copy = rcopy(l1.at[0], l1.at[1], sem_m.at[0, 1], sem_m.at[1, 1], partner)
    go(l_copy)

    def half_rows(which):
        return pl.ds(pl.multiple_of(which * half, half), half)

    def cut(q):
        return pl.ds(q * tile, tile)

    for q in range(n_tile):
        acc[:, q * tile:(q + 1) * tile] = jnp.dot(
            pt[...], tok[:, q * tile:(q + 1) * tile], preferred_element_type=F32
        )
        snd1[q] = acc[half_rows(other), q * tile:(q + 1) * tile].astype(BF16)
        rcopy(snd1.at[q], rcv1.at[q], sem_snd.at[1], sem_1.at[q], partner).start()
    m_copy.wait_recv()
    top_pair = jnp.maximum(m1[0], m1[1])
    shrink = [jnp.exp(m1[i] - top_pair) for i in range(2)]
    for i in range(2):
        fac[i] = column(shrink[i], slots)
    l_copy.wait_recv()
    s2[0, 0] = top_pair
    s2[0, 1] = l1[0] * shrink[0] + l1[1] * shrink[1]
    for r in far_first:
        rcopy(s2.at[0], s2.at[r], sem_snd.at[0], sem_s, peer(r)).start()
    own_fac = fac[0, half_rows(core), :][:, 0:1]
    got_fac = fac[1, half_rows(core), :][:, 0:1]
    for q in range(n_tile):
        landed(rcv1.at[q], sem_1.at[q])
        both = acc[half_rows(core), q * tile:(q + 1) * tile] * own_fac + rcv1[q].astype(F32) * got_fac
        snd2[:, :, q * tile:(q + 1) * tile] = both.reshape(n_chip, rows, tile).astype(BF16)
        for r in far_first:
            rcopy(
                snd2.at[near(r), :, cut(q)], rcv2.at[r, :, cut(q)], sem_snd.at[2], sem_2.at[q], peer(r)
            ).start()

    landed(s2.at[pl.ds(1, n_chip - 1)], sem_s)
    top_all = functools.reduce(jnp.maximum, [s2[r, 0] for r in range(n_chip)])
    factors = [jnp.exp(s2[r, 0] - top_all) for r in range(n_chip)]
    grand = functools.reduce(jnp.add, [s2[r, 1] * factors[r] for r in range(n_chip)])
    wide[...] = jnp.zeros_like(wide)
    for r in range(n_chip):
        wide[r:r + 1, :] = factors[r] / grand
    tot[...] = jnp.transpose(wide[...])
    piece = core * n_chip + chip
    weight = tot[pl.ds(pl.multiple_of(piece * rows, rows), rows), :]
    for q in range(n_tile):
        landed(rcv2.at[pl.ds(1, n_chip - 1), :, cut(q)], sem_2.at[q])
        mine_sum = snd2[chip, :, q * tile:(q + 1) * tile].astype(F32) * weight[:, 0:1]
        for r in range(1, n_chip):
            mine_sum = mine_sum + rcv2[r, :, q * tile:(q + 1) * tile].astype(F32) * weight[:, r:r + 1]
        ag[piece, :, q * tile:(q + 1) * tile] = mine_sum.astype(BF16)
        span = ag.at[piece, :, cut(q)]
        rcopy(span, span, sem_snd.at[4], sem_fw.at[0], partner).start()
        for r in range(mirror - 1, 0, -1):
            rcopy(span, span, sem_snd.at[3], sem_ag.at[r], peer(r)).start()
    for r in range(mirror, n_chip):
        rcopy(ag.at[piece], ag.at[piece], sem_snd.at[3], sem_ag.at[r], peer(r)).start()

    for r in range(1, n_exp):
        emb_copy(r).wait_recv()
        go(emb_relay(r, core))
    win_in.wait()
    wout_in.wait()

    def expert(p):
        e = (p * rows) // slot_exp
        h = gelu_tanh(jnp.dot(ag[p], win[e], preferred_element_type=F32)).astype(BF16)
        return jnp.dot(h, wout[e], preferred_element_type=F32)

    every = pl.ds(0, n_exp)
    cuts = pl.ds(0, n_cut)
    side = n_exp * mirror

    def gather(rs):
        for r in rs:
            p = core * n_chip + near(r)
            if r:
                landed(ag.at[p], sem_ag.at[r])
                rcopy(ag.at[p], ag.at[p], sem_snd.at[4], sem_fw.at[r], partner).start()

    def run_own(rs):
        for r in rs:
            keep[r] = expert(core * n_chip + near(r))

    def run_other(rs):
        for r in rs:
            p = other * n_chip + near(r)
            landed(ag.at[p], sem_fw.at[r])
            snd3[r] = expert(p).astype(BF16)
            rcopy(snd3.at[r], rcv3.at[r], sem_snd.at[5], sem_3.at[r], partner).start()

    def flush(g, rs):
        for r in rs:
            landed(rcv3.at[r], sem_3.at[r])
            y = (keep[r] + rcv3[r].astype(F32)).astype(BF16)
            for q in range(n_exp):
                for h in range(n_cut):
                    low = q * cols + h * wide_cut
                    snd4[g, h, q * mirror + r % mirror] = y[:, low:low + wide_cut]
        for h in range(n_cut):
            for d in range(mirror - 1, -1, -1):
                for s in range(n_exp):
                    if d or s:
                        rcopy(
                            snd4.at[g, h, group_at(s) * mirror + d], rcv4.at[g, h, s * mirror + d],
                            sem_snd.at[6 + g], sem_4.at[g, h], across(d, s),
                        ).start()

    def summed(g, h, s):
        sums = snd4[g, h, mine * mirror].astype(F32) if s == 0 else None
        for d in range(mirror):
            if d or s:
                got = rcv4[g, h, s * mirror + d].astype(F32)
                sums = got if sums is None else sums + got
        return sums

    lower, upper = range(mirror), range(mirror, n_chip)
    gather(lower)
    run_own(lower)
    run_other(lower)
    flush(0, lower)
    gather(upper)
    run_own(upper)
    run_other(upper)
    flush(1, upper)
    for h in range(n_cut):
        landed(rcv4.at[0, h, pl.ds(1, side - 1)], sem_4.at[0, h])
        for s in range(n_exp):
            xs[h, s] = summed(0, h, s).astype(BF16)
        rcopy(xs.at[h], xr.at[h], sem_snd.at[8], sem_x.at[h], peer(mirror)).start()

    step = next(s for s in (384, 256, 128, 64, 32, 16) if count % s == 0)

    def combine(i, carry):
        here = pl.ds(pl.multiple_of(i * step, step), step)
        rows_in = tok[here, :]
        parts = [jnp.dot(rows_in, emb[r], preferred_element_type=F32) for r in range(n_exp)]
        top = jnp.max(functools.reduce(jnp.maximum, parts), axis=1, keepdims=True)
        parts = [jnp.exp(v - top) for v in parts]
        full = jnp.sum(functools.reduce(jnp.add, parts), axis=1, keepdims=True)
        inv = 1.0 / full
        for r in range(n_exp):
            comb[here, r * slots:(r + 1) * slots] = (parts[r] * inv).astype(BF16)
        return carry

    for r in range(1, n_exp):
        emb_relay(r, other).wait_recv()
    n_step = count // step
    early = n_step * 3 // 5
    lax.fori_loop(0, early, combine, 0)

    homed = core * n_chip + near(mirror)

    def span(h, x):
        return so.at[h, every, core * n_chip + near(x)]

    def spread(h, i):
        there = {"seq": (i + (i + n_chip - chip) // n_chip) * 2 + core}
        rcopy(span(h, mirror), span(h, mirror), sem_snd.at[9], sem_a.at[h, near(mirror)], there).start()

    def relay(h, x):
        rcopy(span(h, x), span(h, x), sem_snd.at[10], sem_af.at[h], partner).start()

    for h in range(n_cut):
        landed(rcv4.at[1, h, pl.ds(1, side - 1)], sem_4.at[1, h])
        landed(xr.at[h], sem_x.at[h])
        for s in range(n_exp):
            so[h, s, homed] = (summed(1, h, s) + xr[h, s].astype(F32)).astype(BF16)
        spread(h, 0)
        relay(h, mirror)
    for i in range(1, n_chip - 1):
        for h in range(n_cut):
            spread(h, i)
    lax.fori_loop(early, n_step, combine, 0)
    for h in range(n_cut):
        for x in list(range(mirror + 1, n_chip)) + list(range(mirror)):
            landed(span(h, x), sem_a.at[h, near(x)])
            relay(h, x)
    flat = (n_exp * slots, wide_cut)
    for h in range(n_cut):
        landed(so.at[h, every, pl.ds(other * n_chip, n_chip)], sem_af.at[h])
        for i in range(count // step):
            here = pl.ds(i * step, step)
            table = so[h].reshape(flat) if rows % 16 == 0 else so[h].astype(F32).reshape(flat).astype(BF16)
            mixed = jnp.dot(comb[here, :], table, preferred_element_type=F32).astype(BF16)
            out[here, h * wide_cut:(h + 1) * wide_cut] = mixed
    for cp in pending:
        cp.wait_send()
    drained(s2.at[pl.ds(1, n_chip - 1)], sem_snd.at[0])
    drained(snd1, sem_snd.at[1])
    drained(snd2.at[pl.ds(0, n_chip - 1)], sem_snd.at[2])
    drained(ag.at[pl.ds(0, n_chip - 1)], sem_snd.at[3])
    drained(ag.at[pl.ds(0, n_chip)], sem_snd.at[4])
    drained(snd3, sem_snd.at[5])
    for g in range(2):
        drained(snd4.at[g, cuts, pl.ds(0, side - 1)], sem_snd.at[6 + g])
    drained(xs, sem_snd.at[8])
    drained(so.at[cuts, every, pl.ds(0, n_chip - 1)], sem_snd.at[9])
    drained(so.at[cuts, every, pl.ds(0, n_chip)], sem_snd.at[10])


def solution(mesh):
    n_seq, n_exp = mesh.shape["seq"], mesh.shape["exp"]
    n_chip = n_seq // 2

    def on_device(tokens, slot_embed, w_in, w_out):
        count, features = tokens.shape
        slots = slot_embed.shape[1]
        experts, _, hid = w_in.shape
        slot_exp = slots // experts
        rows = slots // n_seq
        half = slots // 2
        cols = features // n_exp
        n_tile = features // 256
        n_cut = 2 if cols % 256 == 0 else 1
        room = 49 * 1024 * 1024
        dma = pltpu.SemaphoreType.DMA
        vmem = pltpu.VMEM
        anywhere = pl.BlockSpec(memory_space=pltpu.HBM)
        return pl.pallas_call(
            functools.partial(kernel, n_seq, n_exp, slot_exp),
            out_shape=jax.ShapeDtypeStruct((count, cols), BF16),
            in_specs=[anywhere] * 4,
            out_specs=pl.BlockSpec(memory_space=pltpu.VMEM),
            scratch_shapes=[
                vmem((count, features), BF16),
                vmem((n_exp, features, slots), BF16),
                vmem((slots, features), BF16),
                vmem(w_in.shape, BF16),
                vmem(w_out.shape, BF16),
                vmem((slots, count), F32),
                vmem((slots, count), BF16),
                vmem((slots, features), F32),
                vmem((count, n_exp * slots), BF16),
                vmem((2, 1, slots), F32),
                vmem((2, 1, slots), F32),
                vmem((n_chip, 2, 1, slots), F32),
                vmem((2, slots, 128), F32),
                vmem((128, slots), F32),
                vmem((slots, 128), F32),
                vmem((n_tile, half, 256), BF16),
                vmem((n_tile, half, 256), BF16),
                vmem((n_chip, rows, features), BF16),
                vmem((n_chip, rows, features), BF16),
                vmem((n_seq, rows, features), BF16),
                vmem((n_chip, rows, features), F32),
                vmem((n_chip, rows, features), BF16),
                vmem((n_chip, rows, features), BF16),
                vmem((2, n_cut, n_exp * n_chip // 2, rows, cols // n_cut), BF16),
                vmem((2, n_cut, n_exp * n_chip // 2, rows, cols // n_cut), BF16),
                vmem((n_cut, n_exp, rows, cols // n_cut), BF16),
                vmem((n_cut, n_exp, rows, cols // n_cut), BF16),
                vmem((n_cut, n_exp, n_seq, rows, cols // n_cut), BF16),
                dma((-(-count // 512),)),
                dma,
                dma((2,)),
                dma((2, n_exp)),
                dma((2, n_exp)),
                dma((2, 2)),
                dma((11,)),
                dma,
                dma((n_tile,)),
                dma((n_tile,)),
                dma((n_chip,)),
                dma((n_chip,)),
                dma((n_chip,)),
                dma((2, n_cut)),
                dma((n_cut,)),
                dma((n_cut, n_chip)),
                dma((n_cut,)),
            ],
            compiler_params=pltpu.CompilerParams(
                collective_id=0, has_side_effects=True, vmem_limit_bytes=room
            ),
        )(tokens, pltpu.with_memory_space_constraint(slot_embed, pltpu.HBM), w_in, w_out)

    placed = (P("seq", None), P(None, "exp"), P("exp", None, "seq"), P("exp", "seq", None))
    return jax.shard_map(
        on_device, mesh=mesh, in_specs=placed, out_specs=P("seq", "exp"), check_vma=False
    )
```

```python
import functools

import jax
import jax.numpy as jnp
from jax import lax
from jax.experimental import pallas as pl
from jax.experimental.pallas import tpu as pltpu
from jax.sharding import PartitionSpec as P

MESH = pl.DeviceIdType.MESH
F32 = jnp.float32
BF16 = jnp.bfloat16


def gelu_tanh(v):
    return 0.5 * v * (1.0 + jnp.tanh(0.7978845608028654 * (v + 0.044715 * v * v * v)))


def rcopy(src, dst, send, recv, dev):
    return pltpu.make_async_remote_copy(
        src_ref=src, dst_ref=dst, send_sem=send, recv_sem=recv, device_id=dev, device_id_type=MESH
    )


def column(row, slots):
    return jnp.transpose(jnp.broadcast_to(row, (128, slots)))


def kernel(
    n_seq, n_exp, slot_exp, tok_hbm, emb_hbm, win_hbm, wout_hbm, comb, so,
    tok, emb, embt, win, wout, logt, pt, acc, m1, l1, s2, fac, wide, tot,
    snd1, rcv1, snd2, rcv2, ag, keep, snd3, rcv3, snd4, rcv4, xs, xr,
    sem_tok, sem_in, sem_w, sem_emb, sem_er, sem_m, sem_snd,
    sem_s, sem_1, sem_2, sem_ag, sem_fw, sem_3, sem_4, sem_x, sem_a, sem_af,
):
    n_chip = n_seq // 2
    count, features = tok.shape
    slots = embt.shape[0]
    rows = slots // n_seq
    half = slots // 2
    cols = features // n_exp
    tile = features // 2
    n_tile = features // tile
    n_cut = so.shape[0]
    wide_cut = cols // n_cut
    mirror = n_chip // 2
    me = lax.axis_index("seq")
    mine = lax.axis_index("exp")
    chip = me // 2
    core = lax.rem(me, 2)
    other = 1 - core
    partner = {"seq": chip * 2 + other}
    pending = []

    def near(r):
        return chip_ids[r]

    chip_ids = [chip]
    for r in range(1, n_chip):
        mate, bit = chip, 1
        while bit < n_chip:
            if r & bit:
                mate = mate + bit * (1 - 2 * lax.rem(chip // bit, 2))
            bit *= 2
        chip_ids.append(mate)
    far_first = list(range(n_chip - 1, 0, -1))

    def peer(r):
        return {"seq": near(r) * 2 + core}

    def group_at(s):
        return lax.rem(mine + s, n_exp)

    def across(r, s):
        return {"seq": near(r) * 2 + core, "exp": group_at(s)}

    def go(cp):
        cp.start()
        pending.append(cp)

    def landed(view, sem):
        rcopy(view, view, sem, sem, partner).wait_recv()

    def drained(view, sem):
        rcopy(view, view, sem, sem, partner).wait_send()

    emb_in = pltpu.make_async_copy(emb_hbm, emb.at[0], sem_in)
    emb_in.start()
    chunks = []
    at = 0
    while at < count:
        size = count
        cp = pltpu.make_async_copy(tok_hbm.at[pl.ds(at, size)], tok.at[pl.ds(at, size)], sem_tok.at[len(chunks)])
        cp.start()
        chunks.append((at, size, cp))
        at += size

    barrier = pltpu.get_barrier_semaphore()
    for s in range(n_exp):
        for r in range(n_chip):
            if r or s:
                pl.semaphore_signal(barrier, inc=1, device_id=across(r, s), device_id_type=MESH)
    pl.semaphore_signal(barrier, inc=1, device_id=partner, device_id_type=MESH)

    emb_in.wait()
    for q in range(n_tile):
        embt[:, q * tile:(q + 1) * tile] = jnp.transpose(emb[0, q * tile:(q + 1) * tile, :])
    peak = None
    deep = features // 2

    def part_of(which):
        return pl.ds(pl.multiple_of(which * deep, deep), deep)

    def emb_copy(r):
        there = emb.at[r, part_of(core)]
        return rcopy(emb.at[0, part_of(core)], there, sem_emb.at[0, r], sem_emb.at[1, r], {"exp": group_at(r)})

    def emb_relay(r, which):
        there = emb.at[r, part_of(which)]
        return rcopy(there, there, sem_er.at[0, r], sem_er.at[1, r], partner)

    for at, size, cp in chunks:
        cp.wait()
        lt = lax.dot_general(
            embt[...], tok[at:at + size, :], (((1,), (1,)), ((), ())), preferred_element_type=F32
        )
        logt[:, at:at + size] = lt
        top = jnp.max(lt, axis=1, keepdims=True)
        peak = top if peak is None else jnp.maximum(peak, top)
        if at == 0:
            pl.semaphore_wait(barrier, n_chip * n_exp)
            for r in range(1, n_exp):
                go(emb_copy(r))
    win_in = pltpu.make_async_copy(win_hbm, win, sem_w.at[0])
    wout_in = pltpu.make_async_copy(wout_hbm, wout, sem_w.at[1])
    win_in.start()
    wout_in.start()
    m1[0] = jnp.transpose(jnp.broadcast_to(peak, (slots, 128)))[0:1, :]
    m_copy = rcopy(m1.at[0], m1.at[1], sem_m.at[0, 0], sem_m.at[1, 0], partner)
    go(m_copy)

    total = None
    for at, size, _ in chunks:
        w = jnp.exp(logt[:, at:at + size] - peak)
        pt[:, at:at + size] = w.astype(BF16)
        part = jnp.sum(w, axis=1, keepdims=True)
        total = part if total is None else total + part
    l1[0] = jnp.transpose(jnp.broadcast_to(total, (slots, 128)))[0:1, :]
    l_copy = rcopy(l1.at[0], l1.at[1], sem_m.at[0, 1], sem_m.at[1, 1], partner)
    go(l_copy)

    def half_rows(which):
        return pl.ds(pl.multiple_of(which * half, half), half)

    def cut(q):
        return pl.ds(q * tile, tile)

    for q in range(n_tile):
        acc[:, q * tile:(q + 1) * tile] = jnp.dot(
            pt[...], tok[:, q * tile:(q + 1) * tile], preferred_element_type=F32
        )
        snd1[q] = acc[half_rows(other), q * tile:(q + 1) * tile].astype(BF16)
        rcopy(snd1.at[q], rcv1.at[q], sem_snd.at[1], sem_1.at[q], partner).start()
    m_copy.wait_recv()
    top_pair = jnp.maximum(m1[0], m1[1])
    shrink = [jnp.exp(m1[i] - top_pair) for i in range(2)]
    for i in range(2):
        fac[i] = column(shrink[i], slots)
    l_copy.wait_recv()
    s2[0, 0] = top_pair
    s2[0, 1] = l1[0] * shrink[0] + l1[1] * shrink[1]
    for r in far_first:
        rcopy(s2.at[0], s2.at[r], sem_snd.at[0], sem_s, peer(r)).start()
    own_fac = fac[0, half_rows(core), :][:, 0:1]
    got_fac = fac[1, half_rows(core), :][:, 0:1]
    for q in range(n_tile):
        landed(rcv1.at[q], sem_1.at[q])
        both = acc[half_rows(core), q * tile:(q + 1) * tile] * own_fac + rcv1[q].astype(F32) * got_fac
        snd2[:, :, q * tile:(q + 1) * tile] = both.reshape(n_chip, rows, tile).astype(BF16)
        for r in far_first:
            rcopy(
                snd2.at[near(r), :, cut(q)], rcv2.at[r, :, cut(q)], sem_snd.at[2], sem_2.at[q], peer(r)
            ).start()

    landed(s2.at[pl.ds(1, n_chip - 1)], sem_s)
    top_all = functools.reduce(jnp.maximum, [s2[r, 0] for r in range(n_chip)])
    factors = [jnp.exp(s2[r, 0] - top_all) for r in range(n_chip)]
    grand = functools.reduce(jnp.add, [s2[r, 1] * factors[r] for r in range(n_chip)])
    wide[...] = jnp.zeros_like(wide)
    for r in range(n_chip):
        wide[r:r + 1, :] = factors[r] / grand
    tot[...] = jnp.transpose(wide[...])
    piece = core * n_chip + chip
    weight = tot[pl.ds(pl.multiple_of(piece * rows, rows), rows), :]
    for q in range(n_tile):
        landed(rcv2.at[pl.ds(1, n_chip - 1), :, cut(q)], sem_2.at[q])
        mine_sum = snd2[chip, :, q * tile:(q + 1) * tile].astype(F32) * weight[:, 0:1]
        for r in range(1, n_chip):
            mine_sum = mine_sum + rcv2[r, :, q * tile:(q + 1) * tile].astype(F32) * weight[:, r:r + 1]
        ag[piece, :, q * tile:(q + 1) * tile] = mine_sum.astype(BF16)
        span = ag.at[piece, :, cut(q)]
        rcopy(span, span, sem_snd.at[4], sem_fw.at[0], partner).start()
        for r in range(mirror - 1, 0, -1):
            rcopy(span, span, sem_snd.at[3], sem_ag.at[r], peer(r)).start()
    for r in range(mirror, n_chip):
        rcopy(ag.at[piece], ag.at[piece], sem_snd.at[3], sem_ag.at[r], peer(r)).start()

    for r in range(1, n_exp):
        emb_copy(r).wait_recv()
        go(emb_relay(r, core))
    win_in.wait()
    wout_in.wait()

    def expert(p):
        e = (p * rows) // slot_exp
        h = gelu_tanh(jnp.dot(ag[p], win[e], preferred_element_type=F32)).astype(BF16)
        return jnp.dot(h, wout[e], preferred_element_type=F32)

    every = pl.ds(0, n_exp)
    cuts = pl.ds(0, n_cut)
    side = n_exp * mirror

    def gather(rs):
        for r in rs:
            p = core * n_chip + near(r)
            if r:
                landed(ag.at[p], sem_ag.at[r])
                rcopy(ag.at[p], ag.at[p], sem_snd.at[4], sem_fw.at[r], partner).start()

    def run_own(rs):
        for r in rs:
            keep[r] = expert(core * n_chip + near(r))

    def run_other(rs):
        for r in rs:
            p = other * n_chip + near(r)
            landed(ag.at[p], sem_fw.at[r])
            snd3[r] = expert(p).astype(BF16)
            rcopy(snd3.at[r], rcv3.at[r], sem_snd.at[5], sem_3.at[r], partner).start()

    def flush(g, rs):
        for r in rs:
            landed(rcv3.at[r], sem_3.at[r])
            y = (keep[r] + rcv3[r].astype(F32)).astype(BF16)
            for q in range(n_exp):
                for h in range(n_cut):
                    low = q * cols + h * wide_cut
                    snd4[g, h, q * mirror + r % mirror] = y[:, low:low + wide_cut]
        for h in range(n_cut):
            for d in range(mirror - 1, -1, -1):
                for s in range(n_exp):
                    if d or s:
                        rcopy(
                            snd4.at[g, h, group_at(s) * mirror + d], rcv4.at[g, h, s * mirror + d],
                            sem_snd.at[6 + g], sem_4.at[g, h], across(d, s),
                        ).start()

    def summed(g, h, s):
        sums = snd4[g, h, mine * mirror].astype(F32) if s == 0 else None
        for d in range(mirror):
            if d or s:
                got = rcv4[g, h, s * mirror + d].astype(F32)
                sums = got if sums is None else sums + got
        return sums

    lower, upper = range(mirror), range(mirror, n_chip)
    gather(lower)
    run_own(lower)
    run_other(lower)
    flush(0, lower)
    gather(upper)
    run_own(upper)
    run_other(upper)
    flush(1, upper)
    for h in range(n_cut):
        landed(rcv4.at[0, h, pl.ds(1, side - 1)], sem_4.at[0, h])
        for s in range(n_exp):
            xs[h, s] = summed(0, h, s).astype(BF16)
        rcopy(xs.at[h], xr.at[h], sem_snd.at[8], sem_x.at[h], peer(mirror)).start()

    step = next(s for s in (384, 256, 128, 64, 32, 16) if count % s == 0)

    def combine(i, carry):
        here = pl.ds(pl.multiple_of(i * step, step), step)
        rows_in = tok[here, :]
        parts = [jnp.dot(rows_in, emb[r], preferred_element_type=F32) for r in range(n_exp)]
        top = jnp.max(functools.reduce(jnp.maximum, parts), axis=1, keepdims=True)
        parts = [jnp.exp(v - top) for v in parts]
        full = jnp.sum(functools.reduce(jnp.add, parts), axis=1, keepdims=True)
        inv = 1.0 / full
        for r in range(n_exp):
            comb[here, r * slots:(r + 1) * slots] = (parts[r] * inv).astype(BF16)
        return carry

    for r in range(1, n_exp):
        emb_relay(r, other).wait_recv()
    n_step = count // step
    early = n_step * 3 // 5
    lax.fori_loop(0, early, combine, 0)

    homed = core * n_chip + near(mirror)

    def span(h, x):
        return so.at[h, every, core * n_chip + near(x)]

    def spread(h, i):
        there = {"seq": (i + (i + n_chip - chip) // n_chip) * 2 + core}
        rcopy(span(h, mirror), span(h, mirror), sem_snd.at[9], sem_a.at[h, near(mirror)], there).start()

    def relay(h, x):
        rcopy(span(h, x), span(h, x), sem_snd.at[10], sem_af.at[h], partner).start()

    for h in range(n_cut):
        landed(rcv4.at[1, h, pl.ds(1, side - 1)], sem_4.at[1, h])
        landed(xr.at[h], sem_x.at[h])
        for s in range(n_exp):
            so[h, s, homed] = (summed(1, h, s) + xr[h, s].astype(F32)).astype(BF16)
        spread(h, 0)
        relay(h, mirror)
    for i in range(1, n_chip - 1):
        for h in range(n_cut):
            spread(h, i)
    lax.fori_loop(early, n_step, combine, 0)
    for h in range(n_cut):
        for x in list(range(mirror + 1, n_chip)) + list(range(mirror)):
            landed(span(h, x), sem_a.at[h, near(x)])
            relay(h, x)
    for h in range(n_cut):
        landed(so.at[h, every, pl.ds(other * n_chip, n_chip)], sem_af.at[h])
    for cp in pending:
        cp.wait_send()
    drained(s2.at[pl.ds(1, n_chip - 1)], sem_snd.at[0])
    drained(snd1, sem_snd.at[1])
    drained(snd2.at[pl.ds(0, n_chip - 1)], sem_snd.at[2])
    drained(ag.at[pl.ds(0, n_chip - 1)], sem_snd.at[3])
    drained(ag.at[pl.ds(0, n_chip)], sem_snd.at[4])
    drained(snd3, sem_snd.at[5])
    for g in range(2):
        drained(snd4.at[g, cuts, pl.ds(0, side - 1)], sem_snd.at[6 + g])
    drained(xs, sem_snd.at[8])
    drained(so.at[cuts, every, pl.ds(0, n_chip - 1)], sem_snd.at[9])
    drained(so.at[cuts, every, pl.ds(0, n_chip)], sem_snd.at[10])


def mix(step, comb, so, out, buf, sems):
    count, cols = buf.shape
    n_cut, n_exp, n_seq, rows, wide_cut = so.shape
    flat = (n_exp * n_seq * rows, wide_cut)
    copies = []
    for i in range(count // step):
        here = pl.ds(i * step, step)
        for h in range(n_cut):
            table = so[h].reshape(flat) if rows % 16 == 0 else so[h].astype(F32).reshape(flat).astype(BF16)
            mixed = jnp.dot(comb[here, :], table, preferred_element_type=F32).astype(BF16)
            buf[here, h * wide_cut:(h + 1) * wide_cut] = mixed
        cp = pltpu.make_async_copy(buf.at[here], out.at[here], sems.at[i])
        cp.start()
        copies.append(cp)
    for cp in copies:
        cp.wait()


def solution(mesh):
    n_seq, n_exp = mesh.shape["seq"], mesh.shape["exp"]
    n_chip = n_seq // 2

    def on_device(tokens, slot_embed, w_in, w_out):
        count, features = tokens.shape
        slots = slot_embed.shape[1]
        experts, _, hid = w_in.shape
        slot_exp = slots // experts
        rows = slots // n_seq
        half = slots // 2
        cols = features // n_exp
        n_tile = 2
        n_cut = 2 if cols % 256 == 0 else 1
        room = 49 * 1024 * 1024
        dma = pltpu.SemaphoreType.DMA
        vmem = pltpu.VMEM
        anywhere = pl.BlockSpec(memory_space=pltpu.HBM)
        comb, so = pl.pallas_call(
            functools.partial(kernel, n_seq, n_exp, slot_exp),
            out_shape=(
                jax.ShapeDtypeStruct((count, n_exp * slots), BF16),
                jax.ShapeDtypeStruct((n_cut, n_exp, n_seq, rows, cols // n_cut), BF16),
            ),
            in_specs=[anywhere] * 4,
            out_specs=(pl.BlockSpec(memory_space=pltpu.VMEM), pl.BlockSpec(memory_space=pltpu.VMEM)),
            scratch_shapes=[
                vmem((count, features), BF16),
                vmem((n_exp, features, slots), BF16),
                vmem((slots, features), BF16),
                vmem(w_in.shape, BF16),
                vmem(w_out.shape, BF16),
                vmem((slots, count), F32),
                vmem((slots, count), BF16),
                vmem((slots, features), F32),
                vmem((2, 1, slots), F32),
                vmem((2, 1, slots), F32),
                vmem((n_chip, 2, 1, slots), F32),
                vmem((2, slots, 128), F32),
                vmem((128, slots), F32),
                vmem((slots, 128), F32),
                vmem((n_tile, half, features // n_tile), BF16),
                vmem((n_tile, half, features // n_tile), BF16),
                vmem((n_chip, rows, features), BF16),
                vmem((n_chip, rows, features), BF16),
                vmem((n_seq, rows, features), BF16),
                vmem((n_chip, rows, features), F32),
                vmem((n_chip, rows, features), BF16),
                vmem((n_chip, rows, features), BF16),
                vmem((2, n_cut, n_exp * n_chip // 2, rows, cols // n_cut), BF16),
                vmem((2, n_cut, n_exp * n_chip // 2, rows, cols // n_cut), BF16),
                vmem((n_cut, n_exp, rows, cols // n_cut), BF16),
                vmem((n_cut, n_exp, rows, cols // n_cut), BF16),
                dma((1,)),
                dma,
                dma((2,)),
                dma((2, n_exp)),
                dma((2, n_exp)),
                dma((2, 2)),
                dma((11,)),
                dma,
                dma((n_tile,)),
                dma((n_tile,)),
                dma((n_chip,)),
                dma((n_chip,)),
                dma((n_chip,)),
                dma((2, n_cut)),
                dma((n_cut,)),
                dma((n_cut, n_chip)),
                dma((n_cut,)),
            ],
            compiler_params=pltpu.CompilerParams(
                collective_id=0, has_side_effects=True, vmem_limit_bytes=room
            ),
        )(tokens, pltpu.with_memory_space_constraint(slot_embed, pltpu.HBM), w_in, w_out)
        step = next(s for s in (384, 256, 128, 64, 32, 16) if count % s == 0)
        return pl.pallas_call(
            functools.partial(mix, step),
            out_shape=jax.ShapeDtypeStruct((count, cols), BF16),
            in_specs=[pl.BlockSpec(memory_space=pltpu.VMEM)] * 2,
            out_specs=anywhere,
            scratch_shapes=[vmem((count, cols), BF16), dma((count // step,))],
            compiler_params=pltpu.CompilerParams(vmem_limit_bytes=16 * 1024 * 1024),
        )(comb, so)

    placed = (P("seq", None), P(None, "exp"), P("exp", None, "seq"), P("exp", "seq", None))
    return jax.shard_map(
        on_device, mesh=mesh, in_specs=placed, out_specs=P("seq", "exp"), check_vma=False
    )
```

```python
import functools

import jax
import jax.numpy as jnp
from jax import lax
from jax.experimental import pallas as pl
from jax.experimental.pallas import tpu as pltpu
from jax.sharding import PartitionSpec as P

MESH = pl.DeviceIdType.MESH
F32 = jnp.float32
BF16 = jnp.bfloat16


def gelu_tanh(v):
    return 0.5 * v * (1.0 + jnp.tanh(0.7978845608028654 * (v + 0.044715 * v * v * v)))


def rcopy(src, dst, send, recv, dev):
    return pltpu.make_async_remote_copy(
        src_ref=src, dst_ref=dst, send_sem=send, recv_sem=recv, device_id=dev, device_id_type=MESH
    )


def column(row, slots):
    return jnp.transpose(jnp.broadcast_to(row, (128, slots)))


def kernel(
    n_seq, n_exp, slot_exp, tok_hbm, emb_hbm, win_hbm, wout_hbm, comb, so,
    tok, emb, embt, win, wout, logt, pt, acc, m1, l1, s2, fac, wide, tot,
    snd1, rcv1, snd2, rcv2, ag, keep, snd3, rcv3, snd4, rcv4, xs, xr,
    sem_tok, sem_in, sem_w, sem_emb, sem_er, sem_m, sem_snd,
    sem_s, sem_1, sem_2, sem_ag, sem_fw, sem_3, sem_4, sem_x, sem_a, sem_af,
):
    n_chip = n_seq // 2
    count, features = tok.shape
    slots = embt.shape[0]
    rows = slots // n_seq
    half = slots // 2
    cols = features // n_exp
    tile = features // 2
    n_tile = features // tile
    n_cut = so.shape[0]
    wide_cut = cols // n_cut
    mirror = n_chip // 2
    me = lax.axis_index("seq")
    mine = lax.axis_index("exp")
    chip = me // 2
    core = lax.rem(me, 2)
    other = 1 - core
    partner = {"seq": chip * 2 + other}
    pending = []

    def near(r):
        return chip_ids[r]

    chip_ids = [chip]
    for r in range(1, n_chip):
        mate, bit = chip, 1
        while bit < n_chip:
            if r & bit:
                mate = mate + bit * (1 - 2 * lax.rem(chip // bit, 2))
            bit *= 2
        chip_ids.append(mate)
    far_first = list(range(n_chip - 1, 0, -1))

    def peer(r):
        return {"seq": near(r) * 2 + core}

    def group_at(s):
        return lax.rem(mine + s, n_exp)

    def across(r, s):
        return {"seq": near(r) * 2 + core, "exp": group_at(s)}

    def go(cp):
        cp.start()
        pending.append(cp)

    def landed(view, sem):
        rcopy(view, view, sem, sem, partner).wait_recv()

    def drained(view, sem):
        rcopy(view, view, sem, sem, partner).wait_send()

    emb_in = pltpu.make_async_copy(emb_hbm, emb.at[0], sem_in)
    emb_in.start()
    chunks = []
    at = 0
    while at < count:
        size = count
        cp = pltpu.make_async_copy(tok_hbm.at[pl.ds(at, size)], tok.at[pl.ds(at, size)], sem_tok.at[len(chunks)])
        cp.start()
        chunks.append((at, size, cp))
        at += size

    barrier = pltpu.get_barrier_semaphore()
    for s in range(n_exp):
        for r in range(n_chip):
            if r or s:
                pl.semaphore_signal(barrier, inc=1, device_id=across(r, s), device_id_type=MESH)
    pl.semaphore_signal(barrier, inc=1, device_id=partner, device_id_type=MESH)

    emb_in.wait()
    for q in range(n_tile):
        embt[:, q * tile:(q + 1) * tile] = jnp.transpose(emb[0, q * tile:(q + 1) * tile, :])
    peak = None
    deep = features // 2

    def part_of(which):
        return pl.ds(pl.multiple_of(which * deep, deep), deep)

    def emb_copy(r):
        there = emb.at[r, part_of(core)]
        return rcopy(emb.at[0, part_of(core)], there, sem_emb.at[0, r], sem_emb.at[1, r], {"exp": group_at(r)})

    def emb_relay(r, which):
        there = emb.at[r, part_of(which)]
        return rcopy(there, there, sem_er.at[0, r], sem_er.at[1, r], partner)

    for at, size, cp in chunks:
        cp.wait()
        lt = lax.dot_general(
            embt[...], tok[at:at + size, :], (((1,), (1,)), ((), ())), preferred_element_type=F32
        )
        logt[:, at:at + size] = lt
        top = jnp.max(lt, axis=1, keepdims=True)
        peak = top if peak is None else jnp.maximum(peak, top)
        if at == 0:
            pl.semaphore_wait(barrier, n_chip * n_exp)
            for r in range(1, n_exp):
                go(emb_copy(r))
    win_in = pltpu.make_async_copy(win_hbm, win, sem_w.at[0])
    wout_in = pltpu.make_async_copy(wout_hbm, wout, sem_w.at[1])
    win_in.start()
    wout_in.start()
    m1[0] = jnp.transpose(jnp.broadcast_to(peak, (slots, 128)))[0:1, :]
    m_copy = rcopy(m1.at[0], m1.at[1], sem_m.at[0, 0], sem_m.at[1, 0], partner)
    go(m_copy)

    total = None
    for at, size, _ in chunks:
        w = jnp.exp(logt[:, at:at + size] - peak)
        pt[:, at:at + size] = w.astype(BF16)
        part = jnp.sum(w, axis=1, keepdims=True)
        total = part if total is None else total + part
    l_copy = rcopy(l1.at[0], l1.at[1], sem_m.at[0, 1], sem_m.at[1, 1], partner)

    def half_rows(which):
        return pl.ds(pl.multiple_of(which * half, half), half)

    def cut(q):
        return pl.ds(q * tile, tile)

    for q in range(n_tile):
        acc[:, q * tile:(q + 1) * tile] = jnp.dot(
            pt[...], tok[:, q * tile:(q + 1) * tile], preferred_element_type=F32
        )
        snd1[q] = acc[half_rows(other), q * tile:(q + 1) * tile].astype(BF16)
        rcopy(snd1.at[q], rcv1.at[q], sem_snd.at[1], sem_1.at[q], partner).start()
        if q == 0:
            l1[0] = jnp.transpose(jnp.broadcast_to(total, (slots, 128)))[0:1, :]
            go(l_copy)
    m_copy.wait_recv()
    top_pair = jnp.maximum(m1[0], m1[1])
    shrink = [jnp.exp(m1[i] - top_pair) for i in range(2)]
    for i in range(2):
        fac[i] = column(shrink[i], slots)
    l_copy.wait_recv()
    s2[0, 0] = top_pair
    s2[0, 1] = l1[0] * shrink[0] + l1[1] * shrink[1]
    for r in far_first:
        rcopy(s2.at[0], s2.at[r], sem_snd.at[0], sem_s, peer(r)).start()
    own_fac = fac[0, half_rows(core), :][:, 0:1]
    got_fac = fac[1, half_rows(core), :][:, 0:1]
    for q in range(n_tile):
        landed(rcv1.at[q], sem_1.at[q])
        both = acc[half_rows(core), q * tile:(q + 1) * tile] * own_fac + rcv1[q].astype(F32) * got_fac
        snd2[:, :, q * tile:(q + 1) * tile] = both.reshape(n_chip, rows, tile).astype(BF16)
        for r in far_first:
            rcopy(
                snd2.at[near(r), :, cut(q)], rcv2.at[r, :, cut(q)], sem_snd.at[2], sem_2.at[q], peer(r)
            ).start()

    landed(s2.at[pl.ds(1, n_chip - 1)], sem_s)
    top_all = functools.reduce(jnp.maximum, [s2[r, 0] for r in range(n_chip)])
    factors = [jnp.exp(s2[r, 0] - top_all) for r in range(n_chip)]
    grand = functools.reduce(jnp.add, [s2[r, 1] * factors[r] for r in range(n_chip)])
    wide[...] = jnp.zeros_like(wide)
    for r in range(n_chip):
        wide[r:r + 1, :] = factors[r] / grand
    tot[...] = jnp.transpose(wide[...])
    piece = core * n_chip + chip
    weight = tot[pl.ds(pl.multiple_of(piece * rows, rows), rows), :]
    for q in range(n_tile):
        landed(rcv2.at[pl.ds(1, n_chip - 1), :, cut(q)], sem_2.at[q])
        mine_sum = snd2[chip, :, q * tile:(q + 1) * tile].astype(F32) * weight[:, 0:1]
        for r in range(1, n_chip):
            mine_sum = mine_sum + rcv2[r, :, q * tile:(q + 1) * tile].astype(F32) * weight[:, r:r + 1]
        ag[piece, :, q * tile:(q + 1) * tile] = mine_sum.astype(BF16)
        span = ag.at[piece, :, cut(q)]
        rcopy(span, span, sem_snd.at[4], sem_fw.at[0], partner).start()
        for r in range(mirror - 1, 0, -1):
            rcopy(span, span, sem_snd.at[3], sem_ag.at[r], peer(r)).start()
    for r in range(mirror, n_chip):
        rcopy(ag.at[piece], ag.at[piece], sem_snd.at[3], sem_ag.at[r], peer(r)).start()

    for r in range(1, n_exp):
        emb_copy(r).wait_recv()
        go(emb_relay(r, core))
    win_in.wait()
    wout_in.wait()

    def expert(p):
        e = (p * rows) // slot_exp
        h = gelu_tanh(jnp.dot(ag[p], win[e], preferred_element_type=F32)).astype(BF16)
        return jnp.dot(h, wout[e], preferred_element_type=F32)

    every = pl.ds(0, n_exp)
    cuts = pl.ds(0, n_cut)
    side = n_exp * mirror

    def gather(rs):
        for r in rs:
            p = core * n_chip + near(r)
            if r:
                landed(ag.at[p], sem_ag.at[r])
                rcopy(ag.at[p], ag.at[p], sem_snd.at[4], sem_fw.at[r], partner).start()

    def run_own(rs):
        for r in rs:
            keep[r] = expert(core * n_chip + near(r))

    def run_other(rs):
        for r in rs:
            p = other * n_chip + near(r)
            landed(ag.at[p], sem_fw.at[r])
            snd3[r] = expert(p).astype(BF16)
            rcopy(snd3.at[r], rcv3.at[r], sem_snd.at[5], sem_3.at[r], partner).start()

    def flush(g, rs):
        for r in rs:
            landed(rcv3.at[r], sem_3.at[r])
            y = (keep[r] + rcv3[r].astype(F32)).astype(BF16)
            for q in range(n_exp):
                for h in range(n_cut):
                    low = q * cols + h * wide_cut
                    snd4[g, h, q * mirror + r % mirror] = y[:, low:low + wide_cut]
        for h in range(n_cut):
            for d in range(mirror - 1, -1, -1):
                for s in range(n_exp):
                    if d or s:
                        rcopy(
                            snd4.at[g, h, group_at(s) * mirror + d], rcv4.at[g, h, s * mirror + d],
                            sem_snd.at[6 + g], sem_4.at[g, h], across(d, s),
                        ).start()

    def summed(g, h, s):
        sums = snd4[g, h, mine * mirror].astype(F32) if s == 0 else None
        for d in range(mirror):
            if d or s:
                got = rcv4[g, h, s * mirror + d].astype(F32)
                sums = got if sums is None else sums + got
        return sums

    lower, upper = range(mirror), range(mirror, n_chip)
    gather(lower)
    run_own(lower)
    run_other(lower)
    flush(0, lower)
    gather(upper)
    run_own(upper)
    run_other(upper)
    flush(1, upper)
    for h in range(n_cut):
        landed(rcv4.at[0, h, pl.ds(1, side - 1)], sem_4.at[0, h])
        for s in range(n_exp):
            xs[h, s] = summed(0, h, s).astype(BF16)
        rcopy(xs.at[h], xr.at[h], sem_snd.at[8], sem_x.at[h], peer(mirror)).start()

    step = next(s for s in (640, 384, 256, 128, 64, 32, 16) if count % s == 0)

    def combine(i, carry):
        here = pl.ds(pl.multiple_of(i * step, step), step)
        rows_in = tok[here, :]
        parts = [jnp.dot(rows_in, emb[r], preferred_element_type=F32) for r in range(n_exp)]
        top = jnp.max(functools.reduce(jnp.maximum, parts), axis=1, keepdims=True)
        parts = [jnp.exp(v - top) for v in parts]
        full = jnp.sum(functools.reduce(jnp.add, parts), axis=1, keepdims=True)
        inv = 1.0 / full
        for r in range(n_exp):
            comb[here, r * slots:(r + 1) * slots] = (parts[r] * inv).astype(BF16)
        return carry

    for r in range(1, n_exp):
        emb_relay(r, other).wait_recv()
    n_step = count // step
    early = n_step * 3 // 5
    lax.fori_loop(0, early, combine, 0)

    homed = core * n_chip + near(mirror)

    def span(h, x):
        return so.at[h, every, core * n_chip + near(x)]

    def spread(h, i):
        there = {"seq": (i + (i + n_chip - chip) // n_chip) * 2 + core}
        rcopy(span(h, mirror), span(h, mirror), sem_snd.at[9], sem_a.at[h, near(mirror)], there).start()

    def relay(h, x):
        rcopy(span(h, x), span(h, x), sem_snd.at[10], sem_af.at[h], partner).start()

    for h in range(n_cut):
        landed(rcv4.at[1, h, pl.ds(1, side - 1)], sem_4.at[1, h])
        landed(xr.at[h], sem_x.at[h])
        for s in range(n_exp):
            so[h, s, homed] = (summed(1, h, s) + xr[h, s].astype(F32)).astype(BF16)
        spread(h, 0)
        relay(h, mirror)
    for i in range(1, n_chip - 1):
        for h in range(n_cut):
            spread(h, i)
    lax.fori_loop(early, n_step, combine, 0)
    for h in range(n_cut):
        for x in list(range(mirror + 1, n_chip)) + list(range(mirror)):
            landed(span(h, x), sem_a.at[h, near(x)])
            relay(h, x)
    for h in range(n_cut):
        landed(so.at[h, every, pl.ds(other * n_chip, n_chip)], sem_af.at[h])
    for cp in pending:
        cp.wait_send()
    drained(s2.at[pl.ds(1, n_chip - 1)], sem_snd.at[0])
    drained(snd1, sem_snd.at[1])
    drained(snd2.at[pl.ds(0, n_chip - 1)], sem_snd.at[2])
    drained(ag.at[pl.ds(0, n_chip - 1)], sem_snd.at[3])
    drained(ag.at[pl.ds(0, n_chip)], sem_snd.at[4])
    drained(snd3, sem_snd.at[5])
    for g in range(2):
        drained(snd4.at[g, cuts, pl.ds(0, side - 1)], sem_snd.at[6 + g])
    drained(xs, sem_snd.at[8])
    drained(so.at[cuts, every, pl.ds(0, n_chip - 1)], sem_snd.at[9])
    drained(so.at[cuts, every, pl.ds(0, n_chip)], sem_snd.at[10])


def mix(step, comb, so, out, buf, sems):
    count, cols = buf.shape
    n_cut, n_exp, n_seq, rows, wide_cut = so.shape
    flat = (n_exp * n_seq * rows, wide_cut)
    copies = []
    for i in range(count // step):
        here = pl.ds(i * step, step)
        for h in range(n_cut):
            table = so[h].reshape(flat) if rows % 16 == 0 else so[h].astype(F32).reshape(flat).astype(BF16)
            mixed = jnp.dot(comb[here, :], table, preferred_element_type=F32).astype(BF16)
            buf[here, h * wide_cut:(h + 1) * wide_cut] = mixed
        cp = pltpu.make_async_copy(buf.at[here], out.at[here], sems.at[i])
        cp.start()
        copies.append(cp)
    for cp in copies:
        cp.wait()


def solution(mesh):
    n_seq, n_exp = mesh.shape["seq"], mesh.shape["exp"]
    n_chip = n_seq // 2

    def on_device(tokens, slot_embed, w_in, w_out):
        count, features = tokens.shape
        slots = slot_embed.shape[1]
        experts, _, hid = w_in.shape
        slot_exp = slots // experts
        rows = slots // n_seq
        half = slots // 2
        cols = features // n_exp
        n_tile = 2
        n_cut = 2 if cols % 256 == 0 else 1
        room = 49 * 1024 * 1024
        dma = pltpu.SemaphoreType.DMA
        vmem = pltpu.VMEM
        anywhere = pl.BlockSpec(memory_space=pltpu.HBM)
        comb, so = pl.pallas_call(
            functools.partial(kernel, n_seq, n_exp, slot_exp),
            out_shape=(
                jax.ShapeDtypeStruct((count, n_exp * slots), BF16),
                jax.ShapeDtypeStruct((n_cut, n_exp, n_seq, rows, cols // n_cut), BF16),
            ),
            in_specs=[anywhere] * 4,
            out_specs=(pl.BlockSpec(memory_space=pltpu.VMEM), pl.BlockSpec(memory_space=pltpu.VMEM)),
            scratch_shapes=[
                vmem((count, features), BF16),
                vmem((n_exp, features, slots), BF16),
                vmem((slots, features), BF16),
                vmem(w_in.shape, BF16),
                vmem(w_out.shape, BF16),
                vmem((slots, count), F32),
                vmem((slots, count), BF16),
                vmem((slots, features), F32),
                vmem((2, 1, slots), F32),
                vmem((2, 1, slots), F32),
                vmem((n_chip, 2, 1, slots), F32),
                vmem((2, slots, 128), F32),
                vmem((128, slots), F32),
                vmem((slots, 128), F32),
                vmem((n_tile, half, features // n_tile), BF16),
                vmem((n_tile, half, features // n_tile), BF16),
                vmem((n_chip, rows, features), BF16),
                vmem((n_chip, rows, features), BF16),
                vmem((n_seq, rows, features), BF16),
                vmem((n_chip, rows, features), F32),
                vmem((n_chip, rows, features), BF16),
                vmem((n_chip, rows, features), BF16),
                vmem((2, n_cut, n_exp * n_chip // 2, rows, cols // n_cut), BF16),
                vmem((2, n_cut, n_exp * n_chip // 2, rows, cols // n_cut), BF16),
                vmem((n_cut, n_exp, rows, cols // n_cut), BF16),
                vmem((n_cut, n_exp, rows, cols // n_cut), BF16),
                dma((1,)),
                dma,
                dma((2,)),
                dma((2, n_exp)),
                dma((2, n_exp)),
                dma((2, 2)),
                dma((11,)),
                dma,
                dma((n_tile,)),
                dma((n_tile,)),
                dma((n_chip,)),
                dma((n_chip,)),
                dma((n_chip,)),
                dma((2, n_cut)),
                dma((n_cut,)),
                dma((n_cut, n_chip)),
                dma((n_cut,)),
            ],
            compiler_params=pltpu.CompilerParams(
                collective_id=0, has_side_effects=True, vmem_limit_bytes=room
            ),
        )(tokens, pltpu.with_memory_space_constraint(slot_embed, pltpu.HBM), w_in, w_out)
        step = next(s for s in (384, 256, 128, 64, 32, 16) if count % s == 0)
        return pl.pallas_call(
            functools.partial(mix, step),
            out_shape=jax.ShapeDtypeStruct((count, cols), BF16),
            in_specs=[pl.BlockSpec(memory_space=pltpu.VMEM)] * 2,
            out_specs=anywhere,
            scratch_shapes=[vmem((count, cols), BF16), dma((count // step,))],
            compiler_params=pltpu.CompilerParams(vmem_limit_bytes=16 * 1024 * 1024),
        )(comb, so)

    placed = (P("seq", None), P(None, "exp"), P("exp", None, "seq"), P("exp", "seq", None))
    return jax.shard_map(
        on_device, mesh=mesh, in_specs=placed, out_specs=P("seq", "exp"), check_vma=False
    )
```

```python
import functools

import jax
import jax.numpy as jnp
from jax import lax
from jax.experimental import pallas as pl
from jax.experimental.pallas import tpu as pltpu
from jax.sharding import PartitionSpec as P

MESH = pl.DeviceIdType.MESH
F32 = jnp.float32
BF16 = jnp.bfloat16


def gelu_tanh(v):
    return 0.5 * v * (1.0 + jnp.tanh(0.7978845608028654 * (v + 0.044715 * v * v * v)))


def rcopy(src, dst, send, recv, dev):
    return pltpu.make_async_remote_copy(
        src_ref=src, dst_ref=dst, send_sem=send, recv_sem=recv, device_id=dev, device_id_type=MESH
    )


def column(row, slots):
    return jnp.transpose(jnp.broadcast_to(row, (128, slots)))


def kernel(
    n_seq, n_exp, slot_exp, tok_hbm, emb_hbm, win_hbm, wout_hbm, comb, so,
    tok, emb, embt, win, wout, logt, pt, acc, m1, l1, s2, fac, wide, tot,
    snd1, rcv1, snd2, rcv2, ag, keep, snd3, rcv3, snd4, rcv4, xs, xr,
    sem_tok, sem_in, sem_w, sem_emb, sem_er, sem_m, sem_snd,
    sem_s, sem_1, sem_2, sem_ag, sem_fw, sem_3, sem_4, sem_x, sem_a, sem_af,
):
    n_chip = n_seq // 2
    count, features = tok.shape
    slots = embt.shape[0]
    rows = slots // n_seq
    half = slots // 2
    cols = features // n_exp
    tile = features // 2
    n_tile = features // tile
    n_cut = so.shape[0]
    wide_cut = cols // n_cut
    mirror = n_chip // 2
    me = lax.axis_index("seq")
    mine = lax.axis_index("exp")
    chip = me // 2
    core = lax.rem(me, 2)
    other = 1 - core
    partner = {"seq": chip * 2 + other}
    pending = []

    def near(r):
        return chip_ids[r]

    chip_ids = [chip]
    for r in range(1, n_chip):
        mate, bit = chip, 1
        while bit < n_chip:
            if r & bit:
                mate = mate + bit * (1 - 2 * lax.rem(chip // bit, 2))
            bit *= 2
        chip_ids.append(mate)
    far_first = list(range(n_chip - 1, 0, -1))

    def peer(r):
        return {"seq": near(r) * 2 + core}

    def group_at(s):
        return lax.rem(mine + s, n_exp)

    def across(r, s):
        return {"seq": near(r) * 2 + core, "exp": group_at(s)}

    def go(cp):
        cp.start()
        pending.append(cp)

    def landed(view, sem):
        rcopy(view, view, sem, sem, partner).wait_recv()

    def drained(view, sem):
        rcopy(view, view, sem, sem, partner).wait_send()

    emb_in = pltpu.make_async_copy(emb_hbm, emb.at[0], sem_in)
    emb_in.start()
    chunks = []
    at = 0
    while at < count:
        size = count
        cp = pltpu.make_async_copy(tok_hbm.at[pl.ds(at, size)], tok.at[pl.ds(at, size)], sem_tok.at[len(chunks)])
        cp.start()
        chunks.append((at, size, cp))
        at += size

    barrier = pltpu.get_barrier_semaphore()
    for s in range(n_exp):
        for r in range(n_chip):
            if r or s:
                pl.semaphore_signal(barrier, inc=1, device_id=across(r, s), device_id_type=MESH)
    pl.semaphore_signal(barrier, inc=1, device_id=partner, device_id_type=MESH)

    emb_in.wait()
    for q in range(n_tile):
        embt[:, q * tile:(q + 1) * tile] = jnp.transpose(emb[0, q * tile:(q + 1) * tile, :])
    peak = None
    deep = features // 2

    def part_of(which):
        return pl.ds(pl.multiple_of(which * deep, deep), deep)

    def emb_copy(r):
        there = emb.at[r, part_of(core)]
        return rcopy(emb.at[0, part_of(core)], there, sem_emb.at[0, r], sem_emb.at[1, r], {"exp": group_at(r)})

    def emb_relay(r, which):
        there = emb.at[r, part_of(which)]
        return rcopy(there, there, sem_er.at[0, r], sem_er.at[1, r], partner)

    for at, size, cp in chunks:
        cp.wait()
        lt = lax.dot_general(
            embt[...], tok[at:at + size, :], (((1,), (1,)), ((), ())), preferred_element_type=F32
        )
        logt[:, at:at + size] = lt
        top = jnp.max(lt, axis=1, keepdims=True)
        peak = top if peak is None else jnp.maximum(peak, top)
        if at == 0:
            pl.semaphore_wait(barrier, n_chip * n_exp)
            for r in range(1, n_exp):
                go(emb_copy(r))
    win_in = pltpu.make_async_copy(win_hbm, win, sem_w.at[0])
    wout_in = pltpu.make_async_copy(wout_hbm, wout, sem_w.at[1])
    win_in.start()
    wout_in.start()
    m1[0] = jnp.transpose(jnp.broadcast_to(peak, (slots, 128)))[0:1, :]
    m_copy = rcopy(m1.at[0], m1.at[1], sem_m.at[0, 0], sem_m.at[1, 0], partner)
    go(m_copy)

    total = None
    for at, size, _ in chunks:
        w = jnp.exp(logt[:, at:at + size] - peak)
        pt[:, at:at + size] = w.astype(BF16)
        part = jnp.sum(w, axis=1, keepdims=True)
        total = part if total is None else total + part
    l_copy = rcopy(l1.at[0], l1.at[1], sem_m.at[0, 1], sem_m.at[1, 1], partner)

    def half_rows(which):
        return pl.ds(pl.multiple_of(which * half, half), half)

    def cut(q):
        return pl.ds(q * tile, tile)

    for q in range(n_tile):
        acc[:, q * tile:(q + 1) * tile] = jnp.dot(
            pt[...], tok[:, q * tile:(q + 1) * tile], preferred_element_type=F32
        )
        snd1[q] = acc[half_rows(other), q * tile:(q + 1) * tile].astype(BF16)
        rcopy(snd1.at[q], rcv1.at[q], sem_snd.at[1], sem_1.at[q], partner).start()
        if q == 0:
            l1[0] = jnp.transpose(jnp.broadcast_to(total, (slots, 128)))[0:1, :]
            go(l_copy)
    m_copy.wait_recv()
    top_pair = jnp.maximum(m1[0], m1[1])
    shrink = [jnp.exp(m1[i] - top_pair) for i in range(2)]
    for i in range(2):
        fac[i] = column(shrink[i], slots)
    l_copy.wait_recv()
    s2[0, 0] = top_pair
    s2[0, 1] = l1[0] * shrink[0] + l1[1] * shrink[1]
    for r in far_first:
        rcopy(s2.at[0], s2.at[r], sem_snd.at[0], sem_s, peer(r)).start()
    own_fac = fac[0, half_rows(core), :][:, 0:1]
    got_fac = fac[1, half_rows(core), :][:, 0:1]
    for q in range(n_tile):
        landed(rcv1.at[q], sem_1.at[q])
        both = acc[half_rows(core), q * tile:(q + 1) * tile] * own_fac + rcv1[q].astype(F32) * got_fac
        snd2[:, :, q * tile:(q + 1) * tile] = both.reshape(n_chip, rows, tile).astype(BF16)
        for r in far_first:
            rcopy(
                snd2.at[near(r), :, cut(q)], rcv2.at[r, :, cut(q)], sem_snd.at[2], sem_2.at[q], peer(r)
            ).start()

    landed(s2.at[pl.ds(1, n_chip - 1)], sem_s)
    top_all = functools.reduce(jnp.maximum, [s2[r, 0] for r in range(n_chip)])
    factors = [jnp.exp(s2[r, 0] - top_all) for r in range(n_chip)]
    grand = functools.reduce(jnp.add, [s2[r, 1] * factors[r] for r in range(n_chip)])
    wide[...] = jnp.zeros_like(wide)
    for r in range(n_chip):
        wide[r:r + 1, :] = factors[r] / grand
    tot[...] = jnp.transpose(wide[...])
    piece = core * n_chip + chip
    weight = tot[pl.ds(pl.multiple_of(piece * rows, rows), rows), :]
    for q in range(n_tile):
        landed(rcv2.at[pl.ds(1, n_chip - 1), :, cut(q)], sem_2.at[q])
        mine_sum = snd2[chip, :, q * tile:(q + 1) * tile].astype(F32) * weight[:, 0:1]
        for r in range(1, n_chip):
            mine_sum = mine_sum + rcv2[r, :, q * tile:(q + 1) * tile].astype(F32) * weight[:, r:r + 1]
        ag[piece, :, q * tile:(q + 1) * tile] = mine_sum.astype(BF16)
        span = ag.at[piece, :, cut(q)]
        rcopy(span, span, sem_snd.at[4], sem_fw.at[0], partner).start()
        for r in range(mirror - 1, 0, -1):
            rcopy(span, span, sem_snd.at[3], sem_ag.at[r], peer(r)).start()
    for r in range(mirror, n_chip):
        rcopy(ag.at[piece], ag.at[piece], sem_snd.at[3], sem_ag.at[r], peer(r)).start()

    for r in range(1, n_exp):
        emb_copy(r).wait_recv()
        go(emb_relay(r, core))
    win_in.wait()
    wout_in.wait()

    def expert(p):
        e = (p * rows) // slot_exp
        h = gelu_tanh(jnp.dot(ag[p], win[e], preferred_element_type=F32)).astype(BF16)
        return jnp.dot(h, wout[e], preferred_element_type=F32)

    every = pl.ds(0, n_exp)
    cuts = pl.ds(0, n_cut)
    side = n_exp * mirror

    def gather(rs):
        for r in rs:
            p = core * n_chip + near(r)
            if r:
                landed(ag.at[p], sem_ag.at[r])
                rcopy(ag.at[p], ag.at[p], sem_snd.at[4], sem_fw.at[r], partner).start()

    def run_own(rs):
        for r in rs:
            keep[r] = expert(core * n_chip + near(r))

    def run_other(rs):
        for r in rs:
            p = other * n_chip + near(r)
            landed(ag.at[p], sem_fw.at[r])
            snd3[r] = expert(p).astype(BF16)
            rcopy(snd3.at[r], rcv3.at[r], sem_snd.at[5], sem_3.at[r], partner).start()

    def flush(g, rs):
        for r in rs:
            landed(rcv3.at[r], sem_3.at[r])
            y = (keep[r] + rcv3[r].astype(F32)).astype(BF16)
            for q in range(n_exp):
                for h in range(n_cut):
                    low = q * cols + h * wide_cut
                    snd4[g, h, q * mirror + r % mirror] = y[:, low:low + wide_cut]
        for h in range(n_cut):
            for d in range(mirror - 1, -1, -1):
                for s in range(n_exp):
                    if d or s:
                        rcopy(
                            snd4.at[g, h, group_at(s) * mirror + d], rcv4.at[g, h, s * mirror + d],
                            sem_snd.at[6 + g], sem_4.at[g, h], across(d, s),
                        ).start()

    def summed(g, h, s):
        sums = snd4[g, h, mine * mirror].astype(F32) if s == 0 else None
        for d in range(mirror):
            if d or s:
                got = rcv4[g, h, s * mirror + d].astype(F32)
                sums = got if sums is None else sums + got
        return sums

    lower, upper = range(mirror), range(mirror, n_chip)
    gather(lower)
    run_other(lower)
    run_own(lower)
    flush(0, lower)
    gather(upper)
    run_other(upper)
    run_own(upper)
    flush(1, upper)
    for h in range(n_cut):
        landed(rcv4.at[0, h, pl.ds(1, side - 1)], sem_4.at[0, h])
        for s in range(n_exp):
            xs[h, s] = summed(0, h, s).astype(BF16)
        rcopy(xs.at[h], xr.at[h], sem_snd.at[8], sem_x.at[h], peer(mirror)).start()

    step = next(s for s in (640, 384, 256, 128, 64, 32, 16) if count % s == 0)

    def combine(i, carry):
        here = pl.ds(pl.multiple_of(i * step, step), step)
        rows_in = tok[here, :]
        parts = [jnp.dot(rows_in, emb[r], preferred_element_type=F32) for r in range(n_exp)]
        top = jnp.max(functools.reduce(jnp.maximum, parts), axis=1, keepdims=True)
        parts = [jnp.exp(v - top) for v in parts]
        full = jnp.sum(functools.reduce(jnp.add, parts), axis=1, keepdims=True)
        inv = 1.0 / full
        for r in range(n_exp):
            comb[here, r * slots:(r + 1) * slots] = (parts[r] * inv).astype(BF16)
        return carry

    for r in range(1, n_exp):
        emb_relay(r, other).wait_recv()
    n_step = count // step
    early = n_step * 3 // 5
    lax.fori_loop(0, early, combine, 0)

    homed = core * n_chip + near(mirror)

    def span(h, x):
        return so.at[h, every, core * n_chip + near(x)]

    def spread(h, i):
        there = {"seq": (i + (i + n_chip - chip) // n_chip) * 2 + core}
        rcopy(span(h, mirror), span(h, mirror), sem_snd.at[9], sem_a.at[h, near(mirror)], there).start()

    def relay(h, x):
        rcopy(span(h, x), span(h, x), sem_snd.at[10], sem_af.at[h], partner).start()

    for h in range(n_cut):
        landed(rcv4.at[1, h, pl.ds(1, side - 1)], sem_4.at[1, h])
        landed(xr.at[h], sem_x.at[h])
        for s in range(n_exp):
            so[h, s, homed] = (summed(1, h, s) + xr[h, s].astype(F32)).astype(BF16)
        spread(h, 0)
        relay(h, mirror)
    for i in range(1, n_chip - 1):
        for h in range(n_cut):
            spread(h, i)
    lax.fori_loop(early, n_step, combine, 0)
    for h in range(n_cut):
        for x in list(range(mirror + 1, n_chip)) + list(range(mirror)):
            landed(span(h, x), sem_a.at[h, near(x)])
            relay(h, x)
    for h in range(n_cut):
        landed(so.at[h, every, pl.ds(other * n_chip, n_chip)], sem_af.at[h])
    for cp in pending:
        cp.wait_send()
    drained(s2.at[pl.ds(1, n_chip - 1)], sem_snd.at[0])
    drained(snd1, sem_snd.at[1])
    drained(snd2.at[pl.ds(0, n_chip - 1)], sem_snd.at[2])
    drained(ag.at[pl.ds(0, n_chip - 1)], sem_snd.at[3])
    drained(ag.at[pl.ds(0, n_chip)], sem_snd.at[4])
    drained(snd3, sem_snd.at[5])
    for g in range(2):
        drained(snd4.at[g, cuts, pl.ds(0, side - 1)], sem_snd.at[6 + g])
    drained(xs, sem_snd.at[8])
    drained(so.at[cuts, every, pl.ds(0, n_chip - 1)], sem_snd.at[9])
    drained(so.at[cuts, every, pl.ds(0, n_chip)], sem_snd.at[10])


def mix(step, comb, so, out, buf, sems):
    count, cols = buf.shape
    n_cut, n_exp, n_seq, rows, wide_cut = so.shape
    flat = (n_exp * n_seq * rows, wide_cut)
    copies = []
    for i in range(count // step):
        here = pl.ds(i * step, step)
        for h in range(n_cut):
            table = so[h].reshape(flat) if rows % 16 == 0 else so[h].astype(F32).reshape(flat).astype(BF16)
            mixed = jnp.dot(comb[here, :], table, preferred_element_type=F32).astype(BF16)
            buf[here, h * wide_cut:(h + 1) * wide_cut] = mixed
        cp = pltpu.make_async_copy(buf.at[here], out.at[here], sems.at[i])
        cp.start()
        copies.append(cp)
    for cp in copies:
        cp.wait()


def solution(mesh):
    n_seq, n_exp = mesh.shape["seq"], mesh.shape["exp"]
    n_chip = n_seq // 2

    def on_device(tokens, slot_embed, w_in, w_out):
        count, features = tokens.shape
        slots = slot_embed.shape[1]
        experts, _, hid = w_in.shape
        slot_exp = slots // experts
        rows = slots // n_seq
        half = slots // 2
        cols = features // n_exp
        n_tile = 2
        n_cut = 2 if cols % 256 == 0 else 1
        room = 49 * 1024 * 1024
        dma = pltpu.SemaphoreType.DMA
        vmem = pltpu.VMEM
        anywhere = pl.BlockSpec(memory_space=pltpu.HBM)
        comb, so = pl.pallas_call(
            functools.partial(kernel, n_seq, n_exp, slot_exp),
            out_shape=(
                jax.ShapeDtypeStruct((count, n_exp * slots), BF16),
                jax.ShapeDtypeStruct((n_cut, n_exp, n_seq, rows, cols // n_cut), BF16),
            ),
            in_specs=[anywhere] * 4,
            out_specs=(pl.BlockSpec(memory_space=pltpu.VMEM), pl.BlockSpec(memory_space=pltpu.VMEM)),
            scratch_shapes=[
                vmem((count, features), BF16),
                vmem((n_exp, features, slots), BF16),
                vmem((slots, features), BF16),
                vmem(w_in.shape, BF16),
                vmem(w_out.shape, BF16),
                vmem((slots, count), F32),
                vmem((slots, count), BF16),
                vmem((slots, features), F32),
                vmem((2, 1, slots), F32),
                vmem((2, 1, slots), F32),
                vmem((n_chip, 2, 1, slots), F32),
                vmem((2, slots, 128), F32),
                vmem((128, slots), F32),
                vmem((slots, 128), F32),
                vmem((n_tile, half, features // n_tile), BF16),
                vmem((n_tile, half, features // n_tile), BF16),
                vmem((n_chip, rows, features), BF16),
                vmem((n_chip, rows, features), BF16),
                vmem((n_seq, rows, features), BF16),
                vmem((n_chip, rows, features), F32),
                vmem((n_chip, rows, features), BF16),
                vmem((n_chip, rows, features), BF16),
                vmem((2, n_cut, n_exp * n_chip // 2, rows, cols // n_cut), BF16),
                vmem((2, n_cut, n_exp * n_chip // 2, rows, cols // n_cut), BF16),
                vmem((n_cut, n_exp, rows, cols // n_cut), BF16),
                vmem((n_cut, n_exp, rows, cols // n_cut), BF16),
                dma((1,)),
                dma,
                dma((2,)),
                dma((2, n_exp)),
                dma((2, n_exp)),
                dma((2, 2)),
                dma((11,)),
                dma,
                dma((n_tile,)),
                dma((n_tile,)),
                dma((n_chip,)),
                dma((n_chip,)),
                dma((n_chip,)),
                dma((2, n_cut)),
                dma((n_cut,)),
                dma((n_cut, n_chip)),
                dma((n_cut,)),
            ],
            compiler_params=pltpu.CompilerParams(
                collective_id=0, has_side_effects=True, vmem_limit_bytes=room
            ),
        )(tokens, pltpu.with_memory_space_constraint(slot_embed, pltpu.HBM), w_in, w_out)
        step = next(s for s in (384, 256, 128, 64, 32, 16) if count % s == 0)
        return pl.pallas_call(
            functools.partial(mix, step),
            out_shape=jax.ShapeDtypeStruct((count, cols), BF16),
            in_specs=[pl.BlockSpec(memory_space=pltpu.VMEM)] * 2,
            out_specs=anywhere,
            scratch_shapes=[vmem((count, cols), BF16), dma((count // step,))],
            compiler_params=pltpu.CompilerParams(vmem_limit_bytes=16 * 1024 * 1024),
        )(comb, so)

    placed = (P("seq", None), P(None, "exp"), P("exp", None, "seq"), P("exp", "seq", None))
    return jax.shard_map(
        on_device, mesh=mesh, in_specs=placed, out_specs=P("seq", "exp"), check_vma=False
    )
```
